256 devices in a mesh: dp: 2 (over z_hi), seq: 128 (over y, x, z_lo, core).
Axes of the slice: x: 4, y: 4, z: 8 (z_hi: 2, z_lo: 4; z = z_hi * 4 + z_lo), core: 2. Of those that a mesh axis runs over, the one named last changes fastest.
Arguments:
- signal: bfloat16 [2, 262144, 256], P('dp', 'seq'), may hold values from -6 to 6
- gating: bfloat16 [2, 262144, 256], P('dp', 'seq'), may hold values from -6 to 6
- upstream: bfloat16 [2, 262144, 256], P('dp', 'seq'), may hold values from -1.5 to 1.5
- left_factor: bfloat16 [512, 512, 512], P('seq'), may hold values from -0.25 to 0.25
- right_factor: bfloat16 [512, 512, 512], P('seq'), may hold values from -0.25 to 0.25
Outputs:
- output: bfloat16 [2, 262144, 256], P('dp', 'seq')
- grad_gating: bfloat16 [2, 262144, 256], P('dp', 'seq')
- grad_signal: bfloat16 [2, 262144, 256], P('dp', 'seq')
- grad_left: bfloat16 [512, 512, 512], P('seq')
- grad_right: bfloat16 [512, 512, 512], P('seq')
The draws below stay inside these ranges and needn't reach their ends.
All inputs are finite; a program needn't handle non-finite values.
Results may differ from the reference program's by a relative error of at most 0.0075.
Values may be sent and summed in bfloat16 or wider, within the bound.
A program may use at most 64 MiB of HBM per device.

```python
import jax
import jax.numpy as jnp
from jax import lax

D = 256
B2 = 512
B1 = 512
LEN = 262144
SEQS = 2


def shard_levels(stream_key, dims, split, least, largest):
    level = 1.0
    for dim, blocks in split:
        heights = jax.random.uniform(jax.random.fold_in(jax.random.fold_in(stream_key, 6), dim), (blocks,), jnp.float32, least / len(split), largest / len(split))
        level = level * jnp.repeat(jnp.exp(heights), dims[dim] // blocks).reshape((-1,) + (1,) * (len(dims) - 1 - dim))
    return level


def normal_values(rng, extent, spread, bound, shards=(), dtype=jnp.bfloat16):
    array = spread * jax.random.normal(rng, extent, jnp.float32)
    if shards:
        array = array * shard_levels(rng, extent, shards, -0.22, 0.18)
    return jnp.clip(array, -bound, bound).astype(dtype)


def setup_inputs(seed: int = 0) -> dict:
    key_list = jax.random.split(jax.random.key(seed), 6)
    return {
        "signal": normal_values(key_list[0], (SEQS, LEN, D), 1.0, 6.0, ((0, 2), (1, 128))),
        "gating": normal_values(key_list[1], (SEQS, LEN, D), 1.0, 6.0, ((0, 2), (1, 128))),
        "upstream": normal_values(key_list[2], (SEQS, LEN, D), 0.25, 1.5, ((0, 2), (1, 128))),
        "left_factor": normal_values(key_list[3], (B1, B2, B2), B2 ** -0.5, 0.25, ((0, 128),)),
        "right_factor": normal_values(key_list[4], (B2, B1, B1), B1 ** -0.5, 0.25, ((0, 128),)),
    }


def rounded(value):
    return lax.optimization_barrier(value.astype(jnp.bfloat16)).astype(jnp.float32)


def reference(signal, gating, upstream, left_factor, right_factor):
    left_full = left_factor.astype(jnp.float32)
    right_full = right_factor.astype(jnp.float32)
    outputs = []
    grad_gates = []
    grad_signals = []
    left_total = jnp.zeros(left_factor.shape, jnp.float32)
    right_total = jnp.zeros(right_factor.shape, jnp.float32)
    for index in range(SEQS):
        values = signal[index].reshape(B1, B2, D).astype(jnp.float32)
        gate_rows = gating[index].reshape(B1, B2, D).astype(jnp.float32)
        upstream_rows = upstream[index].reshape(B1, B2, D).astype(jnp.float32)
        mixed_rows = rounded(jnp.einsum("ikj,ijd->ikd", left_full, values))
        second = rounded(jnp.einsum("kmi,ikd->mkd", right_full, mixed_rows))
        outputs.append((gate_rows * second).astype(jnp.bfloat16).reshape(LEN, D))
        grad_gates.append((upstream_rows * second).astype(jnp.bfloat16).reshape(LEN, D))
        grad_rows = rounded(upstream_rows * gate_rows)
        right_total = right_total + rounded(jnp.einsum("mkd,ikd->kmi", grad_rows, mixed_rows))
        grad_back = rounded(jnp.einsum("kmi,mkd->ikd", right_full, grad_rows))
        left_total = left_total + rounded(jnp.einsum("ikd,ijd->ikj", grad_back, values))
        grad_signals.append(jnp.einsum("ikj,ikd->ijd", left_full, grad_back).astype(jnp.bfloat16).reshape(LEN, D))
    return (jnp.stack(outputs), jnp.stack(grad_gates), jnp.stack(grad_signals),
            left_total.astype(jnp.bfloat16), right_total.astype(jnp.bfloat16))
```

```python
import jax
import jax.numpy as jnp
from jax import lax
from jax.experimental import pallas as pl
from jax.experimental.pallas import tpu as pltpu
from jax.sharding import PartitionSpec as P

MESH = pl.DeviceIdType.MESH
BF = jnp.bfloat16
F32 = jnp.float32


def position():
    zh = lax.axis_index("dp")
    q = lax.axis_index("seq")
    return zh, q // 8, q % 8


def ring_device(pos, dz, dc):
    zh, yx, zc = pos
    z = (zh * 4 + zc // 2 + dz) % 8
    c = (zc + dc) % 2
    dzc = (z % 4) * 2 + c
    return (z // 4, yx * 8 + dzc), dzc


def plane_device(pos, t):
    zh, yx, zc = pos
    y = (yx // 4 + t // 4) % 4
    x = (yx + t) % 4
    return (zh, (y * 4 + x) * 8 + zc), y * 4 + x


def remote(src, dst, send, recv, device):
    return pltpu.make_async_remote_copy(
        src_ref=src, dst_ref=dst, send_sem=send, recv_sem=recv,
        device_id=device, device_id_type=MESH,
    )


def wait_bytes(ref, sem):
    pltpu.make_async_copy(ref, ref, sem).wait()


def dot(a, b, ca, cb):
    return lax.dot_general(a, b, (((ca,), (cb,)), ((), ())), preferred_element_type=F32)


def pack_matrix():
    r = lax.broadcasted_iota(jnp.int32, (256, 256), 0)
    c = lax.broadcasted_iota(jnp.int32, (256, 256), 1)
    want = ((r // 4) % 4) * 64 + (r // 16) * 4 + r % 4
    return jnp.where(c == want, 1.0, 0.0).astype(BF)


def unpack_matrix():
    r = lax.broadcasted_iota(jnp.int32, (256, 256), 0)
    c = lax.broadcasted_iota(jnp.int32, (256, 256), 1)
    want = ((r // 4) % 16) * 16 + (r % 4) * 4 + r // 64
    return jnp.where(c == want, 1.0, 0.0).astype(BF)


def kernel(
    v_hbm, g_hbm, u_hbm, l_hbm, r_hbm,
    out_hbm, gg_hbm, gs_hbm, gl_hbm, gr_hbm,
    vals, gate, up, left, right, work,
    s2, a2, b2, s1, a1, b1, s4, a4, b4, a3, b3,
    cols, gcols, gleft, gright,
    perm, load, out_sem, xs, xr, zs, zr,
):
    pos = position()
    zh, yx, zc = pos
    other = 1 - zh
    z = zh * 4 + zc // 2

    loads = [
        pltpu.make_async_copy(src, dst, load.at[n])
        for n, (src, dst) in enumerate(
            ((u_hbm, up), (g_hbm, gate), (v_hbm, vals.at[zh]), (l_hbm, left), (r_hbm, right))
        )
    ]
    for copy in loads:
        copy.start()

    barrier = pltpu.get_barrier_semaphore()

    @pl.loop(1, 16)
    def _(t):
        pl.semaphore_signal(
            barrier, inc=1, device_id=ring_device(pos, t // 2, t % 2)[0], device_id_type=MESH
        )
        pl.semaphore_signal(
            barrier, inc=1, device_id=plane_device(pos, t)[0], device_id_type=MESH
        )

    perm[0] = pack_matrix()
    perm[1] = unpack_matrix()
    pl.semaphore_wait(barrier, 30)

    partner, _ = ring_device(pos, 4, 0)
    for n in range(4):
        remote(v_hbm.at[n], vals.at[zh, n], zs.at[0], zr.at[0], partner).start()

    def pack(src, dst):
        for b in range(8):
            rows = jnp.concatenate([src[n, pl.ds(64 * b, 64)] for n in range(4)], axis=0)
            packed = dot(perm[0], rows, 1, 0).astype(BF).reshape(2, 8, 16, 256)
            dst[2 * b] = packed[0]
            dst[2 * b + 1] = packed[1]

    def unpack(src, dst):
        for b in range(8):
            rows = jnp.concatenate(
                [src[:, 2 * b].reshape(128, 256), src[:, 2 * b + 1].reshape(128, 256)], axis=0
            )
            flat = dot(perm[1], rows, 1, 0).astype(BF).reshape(4, 64, 256)
            for n in range(4):
                dst[n, pl.ds(64 * b, 64)] = flat[n]

    def plane_send(src, dst, n):
        pltpu.make_async_copy(src.at[yx], dst.at[:, yx], xr.at[n]).start()

        @pl.loop(1, 16)
        def _(t):
            device, there = plane_device(pos, t)
            remote(src.at[there], dst.at[:, yx], xs.at[n], xr.at[n], device).start()

    def ring_send(src, dst, hops, send, recv):
        for dz, dc in hops:
            device, dzc = ring_device(pos, dz, dc)
            remote(src.at[dzc], dst.at[zc], send, recv, device).start()

    def ring_own(a, b, n, first):
        pltpu.make_async_copy(a.at[zh, zc], b.at[zh, zc], zr.at[first + zh]).start()
        ring_send(
            a.at[zh], b.at[zh], ((2, 0), (6, 0), (2, 1), (6, 1)), zs.at[n], zr.at[first + zh]
        )
        ring_send(
            a.at[zh], b.at[zh], ((1, 0), (7, 0), (1, 1), (7, 1), (0, 1)),
            zs.at[n + 1], zr.at[first + zh],
        )

    def ring_other(a, b, n, first):
        pltpu.make_async_copy(a.at[other, zc], b.at[other, zc], zr.at[first + other]).start()
        ring_send(
            a.at[other], b.at[other], ((1, 0), (7, 0), (1, 1), (7, 1), (0, 1)),
            zs.at[n + 2], zr.at[first + other],
        )

    loads[0].wait()
    loads[1].wait()

    @pl.loop(0, 4)
    def _(n):
        work[n] = (up[n].astype(F32) * gate[n].astype(F32)).astype(BF)

    pack(work, s2)
    plane_send(s2, a2, 0)

    loads[2].wait()
    loads[3].wait()

    def mix(s):
        @pl.loop(0, 4)
        def _(n):
            work[n] = dot(left[n], vals[s, n], 1, 0).astype(BF)

        pack(work, s1.at[s])

    mix(zh)
    plane_send(s1.at[zh], a1.at[zh], 1)

    wait_bytes(a2, xr.at[0])
    pltpu.make_async_copy(a2.at[zc], b2.at[zh, zc], zr.at[1 + zh]).start()
    ring_send(
        a2, b2.at[zh],
        ((4, 0), (4, 1), (3, 0), (5, 0), (3, 1), (5, 1), (2, 0), (6, 0)),
        zs.at[1], zr.at[1 + zh],
    )
    ring_send(
        a2, b2.at[zh],
        ((2, 1), (6, 1), (1, 0), (7, 0), (1, 1), (7, 1), (0, 1)),
        zs.at[2], zr.at[1 + zh],
    )
    wait_bytes(a1.at[0], xr.at[1])
    ring_own(a1, b1, 3, 3)

    wait_bytes(vals.at[0], zr.at[0])
    mix(other)
    plane_send(s1.at[other], a1.at[other], 2)
    wait_bytes(a1.at[0], xr.at[2])
    ring_other(a1, b1, 3, 3)

    loads[4].wait()

    def column_back(s, n):
        wait_bytes(b2.at[0], zr.at[1 + s])
        unpack(b2.at[s], gcols.at[s])

        @pl.loop(0, 4)
        def _(k):
            work[k] = dot(right[k], gcols[s, k], 0, 0).astype(BF)

        pack(work, s4.at[s])
        plane_send(s4.at[s], a4.at[s], n)

    column_back(zh, 3)
    column_back(other, 4)

    def column(s):
        wait_bytes(b1.at[0], zr.at[3 + s])
        unpack(b1.at[s], cols.at[s])

        @pl.loop(0, 4)
        def _(k):
            work[k] = dot(right[k], cols[s, k], 1, 0).astype(BF)

        pack(work, s1.at[s])

    wait_bytes(a4.at[0], xr.at[3])
    ring_own(a4, b4, 6, 5)
    wait_bytes(a4.at[0], xr.at[4])
    ring_other(a4, b4, 6, 5)

    wait_bytes(s1.at[0, pl.ds(0, 15)], xs.at[1])
    wait_bytes(s1.at[0, pl.ds(0, 15)], xs.at[2])
    column(zh)
    column(other)
    far = jnp.where(zc % 2 == 0, 2, 6)
    for r, dz in ((0, 0), (1, 1), (2, far), (3, 7)):
        zd = (z + dz) % 8
        s, lane = zd // 4, pl.ds((zd % 4) * 2, 2)
        pltpu.make_async_copy(s1.at[s, yx, lane], a3.at[lane, yx], xr.at[5]).start()

        @pl.loop(1, 16)
        def _(t):
            device, there = plane_device(pos, t)
            remote(s1.at[s, there, lane], a3.at[lane, yx], xs.at[5], xr.at[5], device).start()

    @pl.loop(0, 4)
    def _(k):
        gright[k] = (
            dot(gcols[0, k], cols[0, k], 1, 1) + dot(gcols[1, k], cols[1, k], 1, 1)
        ).astype(BF)

    store_right = pltpu.make_async_copy(gright, gr_hbm, out_sem.at[0])
    store_right.start()

    wait_bytes(a3, xr.at[5])
    pltpu.make_async_copy(a3.at[zc], b3.at[zc], zr.at[7]).start()
    ring_send(
        a3, b3, ((far, 0), (far, 1), (1, 0), (7, 0), (1, 1), (7, 1), (0, 1)), zs.at[9], zr.at[7]
    )

    for s in (0, 1):
        wait_bytes(b4.at[0], zr.at[5 + s])
        unpack(b4.at[s], cols.at[s])

    @pl.loop(0, 4)
    def _(n):
        work[n] = dot(left[n], cols[zh, n], 0, 0).astype(BF)
        gleft[n] = (
            dot(cols[0, n], vals[0, n], 1, 1) + dot(cols[1, n], vals[1, n], 1, 1)
        ).astype(BF)

    store_left = pltpu.make_async_copy(gleft, gl_hbm, out_sem.at[1])
    store_left.start()
    store_signal = pltpu.make_async_copy(work, gs_hbm, out_sem.at[2])
    store_signal.start()

    wait_bytes(b3, zr.at[7])
    unpack(b3, cols.at[0])

    @pl.loop(0, 4)
    def _(n):
        second = cols[0, n].astype(F32)
        gcols[0, n] = (gate[n].astype(F32) * second).astype(BF)
        gcols[1, n] = (up[n].astype(F32) * second).astype(BF)

    store_out = pltpu.make_async_copy(gcols.at[0], out_hbm, out_sem.at[3])
    store_out.start()
    store_gate = pltpu.make_async_copy(gcols.at[1], gg_hbm, out_sem.at[4])
    store_gate.start()

    wait_bytes(vals.at[0], zs.at[0])
    for n in (0, 3, 4, 5):
        wait_bytes(s1.at[0, pl.ds(0, 15)], xs.at[n])
    wait_bytes(a2, zs.at[1])
    wait_bytes(a2.at[pl.ds(0, 7)], zs.at[2])
    for n in (3, 6):
        wait_bytes(a2.at[pl.ds(0, 4)], zs.at[n])
        wait_bytes(a2.at[pl.ds(0, 5)], zs.at[n + 1])
        wait_bytes(a2.at[pl.ds(0, 5)], zs.at[n + 2])
    wait_bytes(a3.at[pl.ds(0, 7)], zs.at[9])
    for store in (store_right, store_left, store_signal, store_out, store_gate):
        store.wait()


def shards(signal, gating, upstream, left_factor, right_factor):
    rows = (4, 512, 256)
    square = (4, 512, 512)
    sent = (16, 8, 16, 256)
    held = (8, 16, 16, 256)
    hbm = pl.BlockSpec(memory_space=pl.ANY)
    shape = jax.ShapeDtypeStruct
    out = pl.pallas_call(
        kernel,
        out_shape=(shape(rows, BF),) * 3 + (shape(square, BF),) * 2,
        in_specs=[hbm] * 5,
        out_specs=(hbm,) * 5,
        scratch_shapes=[
            pltpu.VMEM((2,) + rows, BF),
            pltpu.VMEM(rows, BF),
            pltpu.VMEM(rows, BF),
            pltpu.VMEM(square, BF),
            pltpu.VMEM(square, BF),
            pltpu.VMEM(rows, BF),
            pltpu.VMEM(sent, BF),
            pltpu.VMEM(held, BF),
            pltpu.VMEM((2,) + held, BF),
            pltpu.VMEM((2,) + sent, BF),
            pltpu.VMEM((2,) + held, BF),
            pltpu.VMEM((2,) + held, BF),
            pltpu.VMEM((2,) + sent, BF),
            pltpu.VMEM((2,) + held, BF),
            pltpu.VMEM((2,) + held, BF),
            pltpu.VMEM(held, BF),
            pltpu.VMEM(held, BF),
            pltpu.VMEM((2,) + rows, BF),
            pltpu.VMEM((2,) + rows, BF),
            pltpu.VMEM(square, BF),
            pltpu.VMEM(square, BF),
            pltpu.VMEM((2, 256, 256), BF),
            pltpu.SemaphoreType.DMA((5,)),
            pltpu.SemaphoreType.DMA((5,)),
            pltpu.SemaphoreType.DMA((6,)),
            pltpu.SemaphoreType.DMA((6,)),
            pltpu.SemaphoreType.DMA((10,)),
            pltpu.SemaphoreType.DMA((8,)),
        ],
        compiler_params=pltpu.CompilerParams(
            collective_id=0, has_side_effects=True, vmem_limit_bytes=60 << 20
        ),
    )(
        signal.reshape(rows), gating.reshape(rows), upstream.reshape(rows),
        left_factor, right_factor,
    )
    return tuple(o.reshape(signal.shape) for o in out[:3]) + tuple(out[3:])


def solution(mesh):
    blocks = (P("dp", "seq", None),) * 3 + (P("seq", None, None),) * 2
    return jax.shard_map(shards, mesh=mesh, in_specs=blocks, out_specs=blocks, check_vma=False)
```

```python
import jax
import jax.numpy as jnp
from jax import lax
from jax.experimental import pallas as pl
from jax.experimental.pallas import tpu as pltpu
from jax.sharding import PartitionSpec as P

MESH = pl.DeviceIdType.MESH
BF = jnp.bfloat16
F32 = jnp.float32


def position():
    zh = lax.axis_index("dp")
    q = lax.axis_index("seq")
    return zh, q // 8, q % 8


def ring_device(pos, dz, dc):
    zh, yx, zc = pos
    z = (zh * 4 + zc // 2 + dz) % 8
    c = (zc + dc) % 2
    return (z // 4, yx * 8 + (z % 4) * 2 + c), ((dz + 1) % 4) * 2 + c


def plane_device(pos, t):
    zh, yx, zc = pos
    y = (yx // 4 + t // 4) % 4
    x = (yx + t) % 4
    return (zh, (y * 4 + x) * 8 + zc), y * 4 + x


def remote(src, dst, send, recv, device):
    return pltpu.make_async_remote_copy(
        src_ref=src, dst_ref=dst, send_sem=send, recv_sem=recv,
        device_id=device, device_id_type=MESH,
    )


def wait_bytes(ref, sem):
    pltpu.make_async_copy(ref, ref, sem).wait()


def dot(a, b, ca, cb):
    return lax.dot_general(a, b, (((ca,), (cb,)), ((), ())), preferred_element_type=F32)


def pack_matrix():
    r = lax.broadcasted_iota(jnp.int32, (256, 256), 0)
    c = lax.broadcasted_iota(jnp.int32, (256, 256), 1)
    want = ((r // 4) % 4) * 64 + (r // 16) * 4 + r % 4
    return jnp.where(c == want, 1.0, 0.0).astype(BF)


def unpack_matrix():
    r = lax.broadcasted_iota(jnp.int32, (256, 256), 0)
    c = lax.broadcasted_iota(jnp.int32, (256, 256), 1)
    want = ((r // 4) % 16) * 16 + (r % 4) * 4 + r // 64
    return jnp.where(c == want, 1.0, 0.0).astype(BF)


def unpack(perm, src, dst):
    for b in range(8):
        rows = jnp.concatenate(
            [src[:, 2 * b].reshape(128, 256), src[:, 2 * b + 1].reshape(128, 256)], axis=0
        )
        flat = dot(perm[1], rows, 1, 0).astype(BF).reshape(4, 64, 256)
        for n in range(4):
            dst[n, pl.ds(64 * b, 64)] = flat[n]


def kernel(
    v_hbm, g_hbm, u_hbm, l_hbm, r_hbm,
    b3, perm, gate, up, gsignal, gleft, gright,
    vals, left, right, work,
    s2, a2, b2, s1, a1, b1, s4, a4, b4, a3,
    cols, gcols, load, xs, xr, zs, zr,
):
    pos = position()
    zh, yx, zc = pos
    other = 1 - zh
    z = zh * 4 + zc // 2
    here = 2 + zc % 2
    lanes = [((j - zc // 2 + 5) % 4) * 2 for j in range(4)]

    loads = [
        pltpu.make_async_copy(src, dst, load.at[n])
        for n, (src, dst) in enumerate(
            ((u_hbm, up), (g_hbm, gate), (v_hbm, vals.at[zh]), (l_hbm, left), (r_hbm, right))
        )
    ]
    for copy in loads:
        copy.start()

    barrier = pltpu.get_barrier_semaphore()

    for dz in (4, 3, 5, 2, 6, 1, 7):
        for dc in (0, 1):
            pl.semaphore_signal(
                barrier, inc=1, device_id=ring_device(pos, dz, dc)[0], device_id_type=MESH
            )
    for t in (10, 11, 14, 9, 6, 2, 8, 15, 13, 7, 5, 12, 3, 4, 1):
        pl.semaphore_signal(barrier, inc=1, device_id=plane_device(pos, t)[0], device_id_type=MESH)
    pl.semaphore_signal(barrier, inc=1, device_id=ring_device(pos, 0, 1)[0], device_id_type=MESH)

    perm[0] = pack_matrix()
    perm[1] = unpack_matrix()
    def pack(src, dst):
        for b in range(8):
            rows = jnp.concatenate([src[n, pl.ds(64 * b, 64)] for n in range(4)], axis=0)
            packed = dot(perm[0], rows, 1, 0).astype(BF).reshape(2, 4, 2, 16, 256)
            for h in range(2):
                for j in range(4):
                    dst[2 * b + h, pl.ds(lanes[j], 2)] = packed[h, j]

    def plane_send(src, dst, n, width=8):
        lane = pl.ds(0, width)
        pltpu.make_async_copy(src.at[yx, lane], dst.at[lane, yx], xr.at[n]).start()

        @pl.loop(1, 16)
        def _(t):
            device, there = plane_device(pos, t)
            remote(src.at[there, lane], dst.at[lane, yx], xs.at[n], xr.at[n], device).start()

    def ring_send(src, dst, hops, send, recv):
        for dz, dc in hops:
            device, lane = ring_device(pos, dz, dc)
            remote(src.at[lane], dst.at[zc], send, recv, device).start()

    def ring_own(a, b, n, first):
        pltpu.make_async_copy(a.at[zh, here], b.at[zh, zc], zr.at[first + zh]).start()
        ring_send(
            a.at[zh], b.at[zh], ((2, 0), (6, 0), (2, 1), (6, 1)), zs.at[n], zr.at[first + zh]
        )
        ring_send(
            a.at[zh], b.at[zh], ((1, 0), (7, 0), (1, 1), (7, 1), (0, 1)),
            zs.at[n + 1], zr.at[first + zh],
        )

    def ring_other(a, b, n, first):
        pltpu.make_async_copy(a.at[other, here], b.at[other, zc], zr.at[first + other]).start()
        ring_send(
            a.at[other], b.at[other], ((1, 0), (7, 0), (1, 1), (7, 1), (0, 1)),
            zs.at[n + 2], zr.at[first + other],
        )

    def mix(s):
        @pl.loop(0, 4)
        def _(n):
            work[n] = dot(left[n], vals[s, n], 1, 0).astype(BF)

        pack(work, s1.at[s])

    def column_back(s):
        unpack(perm, b2.at[s], gcols.at[s])

        @pl.loop(0, 4)
        def _(k):
            work[k] = dot(right[k], gcols[s, k], 0, 0).astype(BF)

        pack(work, s4.at[s])

    def column(s):
        wait_bytes(b1.at[0], zr.at[3 + s])
        unpack(perm, b1.at[s], cols.at[s])

        @pl.loop(0, 4)
        def _(k):
            work[k] = dot(right[k], cols[s, k], 1, 0).astype(BF)

        pack(work, s1.at[s])

    loads[0].wait()
    loads[1].wait()

    @pl.loop(0, 4)
    def _(n):
        work[n] = (up[n].astype(F32) * gate[n].astype(F32)).astype(BF)

    pack(work, s2)
    pl.semaphore_wait(barrier, 30)
    partner, _ = ring_device(pos, 4, 0)

    def share_signal(first, last):
        for n in range(first, last):
            remote(v_hbm.at[n], vals.at[zh, n], zs.at[0], zr.at[0], partner).start()

    share_signal(0, 2)
    plane_send(s2, a2, 0)

    loads[2].wait()
    loads[3].wait()
    mix(zh)
    plane_send(s1.at[zh], a1.at[zh], 1)

    wait_bytes(a2, xr.at[0])
    pltpu.make_async_copy(a2.at[here], b2.at[zh, zc], zr.at[1 + zh]).start()
    ring_send(
        a2, b2.at[zh],
        ((4, 0), (4, 1), (3, 0), (5, 0), (3, 1), (5, 1), (2, 0), (6, 0)),
        zs.at[1], zr.at[1 + zh],
    )
    ring_send(
        a2, b2.at[zh],
        ((2, 1), (6, 1), (1, 0), (7, 0), (1, 1), (7, 1), (0, 1)),
        zs.at[2], zr.at[1 + zh],
    )
    share_signal(2, 4)
    wait_bytes(a1.at[0], xr.at[1])
    ring_own(a1, b1, 3, 3)

    loads[4].wait()
    wait_bytes(b2.at[0], zr.at[1 + zh])
    column_back(zh)
    plane_send(s4.at[zh], a4.at[zh], 3)
    wait_bytes(b2.at[0], zr.at[1 + other])
    column_back(other)
    plane_send(s4.at[other], a4.at[other], 4, 6)

    wait_bytes(vals.at[0], zr.at[0])
    mix(other)
    plane_send(s1.at[other], a1.at[other], 2, 6)
    wait_bytes(a1.at[0, pl.ds(0, 6)], xr.at[2])
    ring_other(a1, b1, 3, 3)
    wait_bytes(a4.at[0], xr.at[3])
    ring_own(a4, b4, 6, 5)
    wait_bytes(a4.at[0, pl.ds(0, 6)], xr.at[4])
    ring_other(a4, b4, 6, 5)

    wait_bytes(s1.at[0, pl.ds(0, 15)], xs.at[1])
    wait_bytes(s1.at[0, pl.ds(0, 15), pl.ds(0, 6)], xs.at[2])
    wait_bytes(s1.at[0, pl.ds(0, 15)], xs.at[0])
    column(zh)
    column(other)
    far = jnp.where(zc % 2 == 0, 2, 6)
    for p, dz in enumerate((7, 0, 1, far)):
        s = ((z + dz) % 8) // 4
        s2[:, 2 * p:2 * p + 2] = s1[s, :, 2 * p:2 * p + 2]
    plane_send(s2, a3, 5)

    @pl.loop(0, 4)
    def _(k):
        gright[k] = (
            dot(gcols[0, k], cols[0, k], 1, 1) + dot(gcols[1, k], cols[1, k], 1, 1)
        ).astype(BF)

    wait_bytes(a3, xr.at[5])
    pltpu.make_async_copy(a3.at[here], b3.at[zc], zr.at[7]).start()
    ring_send(
        a3, b3, ((far, 0), (far, 1), (1, 0), (7, 0), (1, 1), (7, 1), (0, 1)), zs.at[9], zr.at[7]
    )

    for s in (0, 1):
        wait_bytes(b4.at[0], zr.at[5 + s])
        unpack(perm, b4.at[s], cols.at[s])

    @pl.loop(0, 4)
    def _(n):
        gsignal[n] = dot(left[n], cols[zh, n], 0, 0).astype(BF)
        gleft[n] = (
            dot(cols[0, n], vals[0, n], 1, 1) + dot(cols[1, n], vals[1, n], 1, 1)
        ).astype(BF)

    wait_bytes(b3, zr.at[7])
    wait_bytes(vals.at[0], zs.at[0])
    for n in (3, 5):
        wait_bytes(s1.at[0, pl.ds(0, 15)], xs.at[n])
    wait_bytes(s1.at[0, pl.ds(0, 15), pl.ds(0, 6)], xs.at[4])
    wait_bytes(a2, zs.at[1])
    wait_bytes(a2.at[pl.ds(0, 7)], zs.at[2])
    for n in (3, 6):
        wait_bytes(a2.at[pl.ds(0, 4)], zs.at[n])
        wait_bytes(a2.at[pl.ds(0, 5)], zs.at[n + 1])
        wait_bytes(a2.at[pl.ds(0, 5)], zs.at[n + 2])
    wait_bytes(a3.at[pl.ds(0, 7)], zs.at[9])


def last_kernel(
    b3, perm, gate, up, gsignal, gleft, gright,
    out_hbm, gg_hbm, gs_hbm, gl_hbm, gr_hbm,
    second, out, ggate, sem, out_sem,
):
    copies = [
        pltpu.make_async_copy(src, dst, sem.at[n])
        for n, (src, dst) in enumerate(((gright, gr_hbm), (gleft, gl_hbm), (gsignal, gs_hbm)))
    ]
    for copy in copies:
        copy.start()
    unpack(perm, b3, second)
    for n in range(4):
        wide = second[n].astype(F32)
        out[n] = (gate[n].astype(F32) * wide).astype(BF)
        ggate[n] = (up[n].astype(F32) * wide).astype(BF)
        for k, (src, dst) in enumerate(((out, out_hbm), (ggate, gg_hbm))):
            copies.append(pltpu.make_async_copy(src.at[n], dst.at[n], out_sem.at[k, n]))
            copies[-1].start()
    for copy in copies:
        copy.wait()


def shards(signal, gating, upstream, left_factor, right_factor):
    rows = (4, 512, 256)
    square = (4, 512, 512)
    sent = (16, 8, 16, 256)
    held = (8, 16, 16, 256)
    hbm = pl.BlockSpec(memory_space=pl.ANY)
    vmem = pl.BlockSpec(memory_space=pltpu.VMEM)
    shape = jax.ShapeDtypeStruct
    last = pl.pallas_call(
        kernel,
        out_shape=(
            pltpu.VMEM(held, BF),
            pltpu.VMEM((2, 256, 256), BF),
            pltpu.VMEM(rows, BF),
            pltpu.VMEM(rows, BF),
            pltpu.VMEM(rows, BF),
            pltpu.VMEM(square, BF),
            pltpu.VMEM(square, BF),
        ),
        in_specs=[hbm] * 5,
        out_specs=(vmem,) * 7,
        scratch_shapes=[
            pltpu.VMEM((2,) + rows, BF),
            pltpu.VMEM(square, BF),
            pltpu.VMEM(square, BF),
            pltpu.VMEM(rows, BF),
            pltpu.VMEM(sent, BF),
            pltpu.VMEM(held, BF),
            pltpu.VMEM((2,) + held, BF),
            pltpu.VMEM((2,) + sent, BF),
            pltpu.VMEM((2,) + held, BF),
            pltpu.VMEM((2,) + held, BF),
            pltpu.VMEM((2,) + sent, BF),
            pltpu.VMEM((2,) + held, BF),
            pltpu.VMEM((2,) + held, BF),
            pltpu.VMEM(held, BF),
            pltpu.VMEM((2,) + rows, BF),
            pltpu.VMEM((2,) + rows, BF),
            pltpu.SemaphoreType.DMA((5,)),
            pltpu.SemaphoreType.DMA((6,)),
            pltpu.SemaphoreType.DMA((6,)),
            pltpu.SemaphoreType.DMA((10,)),
            pltpu.SemaphoreType.DMA((8,)),
        ],
        compiler_params=pltpu.CompilerParams(
            collective_id=0, has_side_effects=True, vmem_limit_bytes=46 << 20
        ),
    )(
        signal.reshape(rows), gating.reshape(rows), upstream.reshape(rows),
        left_factor, right_factor,
    )
    out = pl.pallas_call(
        last_kernel,
        out_shape=(shape(rows, BF),) * 3 + (shape(square, BF),) * 2,
        in_specs=[vmem] * 7,
        out_specs=(hbm,) * 5,
        scratch_shapes=[
            pltpu.VMEM(rows, BF),
            pltpu.VMEM(rows, BF),
            pltpu.VMEM(rows, BF),
            pltpu.SemaphoreType.DMA((3,)),
            pltpu.SemaphoreType.DMA((2, 4)),
        ],
        compiler_params=pltpu.CompilerParams(vmem_limit_bytes=8 << 20),
    )(*[pltpu.with_memory_space_constraint(o, pltpu.VMEM) for o in last])
    return tuple(o.reshape(signal.shape) for o in out[:3]) + tuple(out[3:])


def solution(mesh):
    blocks = (P("dp", "seq", None),) * 3 + (P("seq", None, None),) * 2
    return jax.shard_map(shards, mesh=mesh, in_specs=blocks, out_specs=blocks, check_vma=False)
```

```python
import jax
import jax.numpy as jnp
from jax import lax
from jax.experimental import pallas as pl
from jax.experimental.pallas import tpu as pltpu
from jax.sharding import PartitionSpec as P

MESH = pl.DeviceIdType.MESH
BF = jnp.bfloat16
F32 = jnp.float32


def position():
    zh = lax.axis_index("dp")
    q = lax.axis_index("seq")
    return zh, q // 8, q % 8


def ring_device(pos, dz, dc):
    zh, yx, zc = pos
    z = (zh * 4 + zc // 2 + dz) % 8
    c = (zc + dc) % 2
    return (z // 4, yx * 8 + (z % 4) * 2 + c), ((dz + 1) % 4) * 2 + c


def plane_device(pos, t):
    zh, yx, zc = pos
    y = (yx // 4 + t // 4) % 4
    x = (yx + t) % 4
    return (zh, (y * 4 + x) * 8 + zc), y * 4 + x


def remote(src, dst, send, recv, device):
    return pltpu.make_async_remote_copy(
        src_ref=src, dst_ref=dst, send_sem=send, recv_sem=recv,
        device_id=device, device_id_type=MESH,
    )


def wait_bytes(ref, sem):
    pltpu.make_async_copy(ref, ref, sem).wait()


def dot(a, b, ca, cb):
    return lax.dot_general(a, b, (((ca,), (cb,)), ((), ())), preferred_element_type=F32)


def pack_matrix():
    r = lax.broadcasted_iota(jnp.int32, (256, 256), 0)
    c = lax.broadcasted_iota(jnp.int32, (256, 256), 1)
    want = ((r // 4) % 4) * 64 + (r // 16) * 4 + r % 4
    return jnp.where(c == want, 1.0, 0.0).astype(BF)


def unpack_matrix():
    r = lax.broadcasted_iota(jnp.int32, (256, 256), 0)
    c = lax.broadcasted_iota(jnp.int32, (256, 256), 1)
    want = ((r // 4) % 16) * 16 + (r % 4) * 4 + r // 64
    return jnp.where(c == want, 1.0, 0.0).astype(BF)


def unpack(perm, src, dst):
    for b in range(8):
        rows = jnp.concatenate(
            [src[:, 2 * b].reshape(128, 256), src[:, 2 * b + 1].reshape(128, 256)], axis=0
        )
        flat = dot(perm[1], rows, 1, 0).astype(BF).reshape(4, 64, 256)
        for n in range(4):
            dst[n, pl.ds(64 * b, 64)] = flat[n]


def kernel(
    v_hbm, g_hbm, u_hbm, l_hbm, r_hbm,
    b3, perm, gate, up, gsignal, gleft, gright,
    vals, left, right, work, mixed,
    s2, a2, b2, s1, a1, b1, s4, a4, b4, a3,
    cols, gcols, load, xs, xr, zs, zr,
):
    pos = position()
    zh, yx, zc = pos
    other = 1 - zh
    z = zh * 4 + zc // 2
    here = 2 + zc % 2
    lanes = [((j - zc // 2 + 5) % 4) * 2 for j in range(4)]

    loads = [
        pltpu.make_async_copy(src, dst, load.at[n])
        for n, (src, dst) in enumerate(
            ((u_hbm, up), (g_hbm, gate), (v_hbm, vals.at[zh]), (l_hbm, left), (r_hbm, right))
        )
    ]
    for copy in loads:
        copy.start()

    barrier = pltpu.get_barrier_semaphore()

    for dz in (4, 3, 5, 2, 6, 1, 7):
        for dc in (0, 1):
            pl.semaphore_signal(
                barrier, inc=1, device_id=ring_device(pos, dz, dc)[0], device_id_type=MESH
            )
    for t in (10, 11, 14, 9, 6, 2, 8, 15, 13, 7, 5, 12, 3, 4, 1):
        pl.semaphore_signal(barrier, inc=1, device_id=plane_device(pos, t)[0], device_id_type=MESH)
    pl.semaphore_signal(barrier, inc=1, device_id=ring_device(pos, 0, 1)[0], device_id_type=MESH)

    perm[0] = pack_matrix()
    perm[1] = unpack_matrix()
    def pack(src, dst, half=None):
        for b in range(8):
            rows = jnp.concatenate([src[n, pl.ds(64 * b, 64)] for n in range(4)], axis=0)
            packed = dot(perm[0], rows, 1, 0).astype(BF).reshape(2, 4, 2, 16, 256)
            for h in range(2):
                for j in range(4):
                    if half is None:
                        dst[2 * b + h, pl.ds(lanes[j], 2)] = packed[h, j]
                    else:
                        dst[half[j], 2 * b + h, pl.ds(lanes[j], 2)] = packed[h, j]

    def plane_send(src, dst, n, width=8):
        lane = pl.ds(0, width)
        pltpu.make_async_copy(src.at[yx, lane], dst.at[lane, yx], xr.at[n]).start()

        for t in (10, 5, 15, 7, 13, 1, 4, 3, 12, 6, 9, 14, 11, 2, 8):
            device, there = plane_device(pos, t)
            remote(src.at[there, lane], dst.at[lane, yx], xs.at[n], xr.at[n], device).start()

    def ring_send(src, dst, hops, send, recv):
        for dz, dc in hops:
            device, lane = ring_device(pos, dz, dc)
            remote(src.at[lane], dst.at[zc], send, recv, device).start()

    def ring_near(a, b, n, first):
        pltpu.make_async_copy(a.at[zh, here], b.at[zh, zc], zr.at[first + zh]).start()
        ring_send(
            a.at[zh], b.at[zh], ((1, 0), (7, 0), (1, 1), (7, 1), (0, 1)),
            zs.at[n + 1], zr.at[first + zh],
        )

    def ring_far(a, b, n, first):
        ring_send(
            a.at[zh], b.at[zh], ((2, 0), (6, 0), (2, 1), (6, 1)), zs.at[n], zr.at[first + zh]
        )

    def ring_other(a, b, n, first):
        pltpu.make_async_copy(a.at[other, here], b.at[other, zc], zr.at[first + other]).start()
        ring_send(
            a.at[other], b.at[other], ((1, 0), (7, 0), (1, 1), (7, 1), (0, 1)),
            zs.at[n + 2], zr.at[first + other],
        )

    def mix(s, dst, first, last):
        @pl.loop(first, last)
        def _(n):
            dst[n] = dot(left[n], vals[s, n], 1, 0).astype(BF)

    def column_back(s):
        unpack(perm, b2.at[s], gcols.at[s])

        @pl.loop(0, 4)
        def _(k):
            work[k] = dot(right[k], gcols[s, k], 0, 0).astype(BF)

        pack(work, s4.at[s])

    def column(s):
        wait_bytes(b1.at[0], zr.at[3 + s])
        unpack(perm, b1.at[s], cols.at[s])

        @pl.loop(0, 4)
        def _(k):
            work[k] = dot(right[k], cols[s, k], 1, 0).astype(BF)

        pack(work, s1, [jnp.where(w == s, 0, 1) for w in wanted])

    loads[0].wait()
    loads[1].wait()

    @pl.loop(0, 4)
    def _(n):
        work[n] = (up[n].astype(F32) * gate[n].astype(F32)).astype(BF)

    pack(work, s2)
    pl.semaphore_wait(barrier, 30)
    partner, _ = ring_device(pos, 4, 0)

    def share_signal(first, last):
        for n in range(first, last):
            remote(v_hbm.at[n], vals.at[zh, n], zs.at[0], zr.at[8 * (n // 2)], partner).start()

    share_signal(0, 2)
    plane_send(s2, a2, 0)

    loads[2].wait()
    loads[3].wait()
    mix(zh, work, 0, 4)
    pack(work, s1.at[zh])
    plane_send(s1.at[zh], a1.at[zh], 1)

    wait_bytes(a2, xr.at[0])
    pltpu.make_async_copy(a2.at[here], b2.at[zh, zc], zr.at[1 + zh]).start()
    ring_send(
        a2, b2.at[zh],
        ((4, 0), (4, 1), (3, 0), (5, 0), (3, 1), (5, 1), (2, 0), (6, 0)),
        zs.at[1], zr.at[1 + zh],
    )
    ring_send(
        a2, b2.at[zh],
        ((2, 1), (6, 1), (1, 0), (7, 0), (1, 1), (7, 1), (0, 1)),
        zs.at[2], zr.at[1 + zh],
    )
    share_signal(2, 4)
    wait_bytes(a1.at[0], xr.at[1])
    ring_far(a1, b1, 3, 3)
    ring_near(a1, b1, 3, 3)

    loads[4].wait()
    wait_bytes(b2.at[0], zr.at[1 + zh])
    column_back(zh)
    plane_send(s4.at[zh], a4.at[zh], 3)
    wait_bytes(b2.at[0], zr.at[1 + other])
    column_back(other)
    plane_send(s4.at[other], a4.at[other], 4, 6)

    wait_bytes(vals.at[0, pl.ds(0, 2)], zr.at[0])
    mix(other, mixed, 0, 2)
    wait_bytes(vals.at[0, pl.ds(0, 2)], zr.at[8])
    mix(other, mixed, 2, 4)
    pack(mixed, s1.at[other])
    plane_send(s1.at[other], a1.at[other], 2, 6)
    wait_bytes(a1.at[0, pl.ds(0, 6)], xr.at[2])
    ring_other(a1, b1, 3, 3)
    wait_bytes(a4.at[0], xr.at[3])
    ring_far(a4, b4, 6, 5)
    ring_near(a4, b4, 6, 5)
    wait_bytes(a4.at[0, pl.ds(0, 6)], xr.at[4])
    ring_other(a4, b4, 6, 5)

    wait_bytes(s1.at[0, pl.ds(0, 15)], xs.at[1])
    wait_bytes(s1.at[0, pl.ds(0, 15), pl.ds(0, 6)], xs.at[2])
    far = jnp.where(zc % 2 == 0, 2, 6)
    wanted = []
    for j in range(4):
        hop = (j - zc // 2 + 4) % 4
        hop = jnp.where(hop == 2, far, jnp.where(hop == 3, 7, hop))
        wanted.append(((z + hop) % 8) // 4)
    column(zh)
    column(other)
    plane_send(s1.at[0], a3, 5)

    @pl.loop(0, 4)
    def _(k):
        gright[k] = (
            dot(gcols[0, k], cols[0, k], 1, 1) + dot(gcols[1, k], cols[1, k], 1, 1)
        ).astype(BF)

    wait_bytes(a3, xr.at[5])
    pltpu.make_async_copy(a3.at[here], b3.at[zc], zr.at[7]).start()
    ring_send(
        a3, b3, ((far, 0), (far, 1), (1, 0), (7, 0), (1, 1), (7, 1), (0, 1)), zs.at[9], zr.at[7]
    )

    for s in (0, 1):
        wait_bytes(b4.at[0], zr.at[5 + s])
        unpack(perm, b4.at[s], cols.at[s])

    @pl.loop(0, 4)
    def _(n):
        gsignal[n] = dot(left[n], cols[zh, n], 0, 0).astype(BF)
        gleft[n] = (
            dot(cols[0, n], vals[0, n], 1, 1) + dot(cols[1, n], vals[1, n], 1, 1)
        ).astype(BF)

    wait_bytes(b3, zr.at[7])
    wait_bytes(vals.at[0], zs.at[0])
    for n in (0, 3, 5):
        wait_bytes(s1.at[0, pl.ds(0, 15)], xs.at[n])
    wait_bytes(s1.at[0, pl.ds(0, 15), pl.ds(0, 6)], xs.at[4])
    wait_bytes(a2, zs.at[1])
    wait_bytes(a2.at[pl.ds(0, 7)], zs.at[2])
    for n in (3, 6):
        wait_bytes(a2.at[pl.ds(0, 4)], zs.at[n])
        wait_bytes(a2.at[pl.ds(0, 5)], zs.at[n + 1])
        wait_bytes(a2.at[pl.ds(0, 5)], zs.at[n + 2])
    wait_bytes(a3.at[pl.ds(0, 7)], zs.at[9])


def last_kernel(
    b3, perm, gate, up, gsignal, gleft, gright,
    out_hbm, gg_hbm, gs_hbm, gl_hbm, gr_hbm,
    second, out, ggate, sem, out_sem,
):
    copies = [
        pltpu.make_async_copy(src.at[k], dst.at[k], sem.at[n, k])
        for n, (src, dst) in enumerate(((gright, gr_hbm), (gleft, gl_hbm), (gsignal, gs_hbm)))
        for k in range(4)
    ]
    for copy in copies:
        copy.start()
    unpack(perm, b3, second)
    for n in range(4):
        wide = second[n].astype(F32)
        out[n] = (gate[n].astype(F32) * wide).astype(BF)
        ggate[n] = (up[n].astype(F32) * wide).astype(BF)
        for k, (src, dst) in enumerate(((out, out_hbm), (ggate, gg_hbm))):
            copies.append(pltpu.make_async_copy(src.at[n], dst.at[n], out_sem.at[k, n]))
            copies[-1].start()
    for copy in copies:
        copy.wait()


def shards(signal, gating, upstream, left_factor, right_factor):
    rows = (4, 512, 256)
    square = (4, 512, 512)
    sent = (16, 8, 16, 256)
    held = (8, 16, 16, 256)
    hbm = pl.BlockSpec(memory_space=pl.ANY)
    vmem = pl.BlockSpec(memory_space=pltpu.VMEM)
    shape = jax.ShapeDtypeStruct
    last = pl.pallas_call(
        kernel,
        out_shape=(
            pltpu.VMEM(held, BF),
            pltpu.VMEM((2, 256, 256), BF),
            pltpu.VMEM(rows, BF),
            pltpu.VMEM(rows, BF),
            pltpu.VMEM(rows, BF),
            pltpu.VMEM(square, BF),
            pltpu.VMEM(square, BF),
        ),
        in_specs=[hbm] * 5,
        out_specs=(vmem,) * 7,
        scratch_shapes=[
            pltpu.VMEM((2,) + rows, BF),
            pltpu.VMEM(square, BF),
            pltpu.VMEM(square, BF),
            pltpu.VMEM(rows, BF),
            pltpu.VMEM(rows, BF),
            pltpu.VMEM(sent, BF),
            pltpu.VMEM(held, BF),
            pltpu.VMEM((2,) + held, BF),
            pltpu.VMEM((2,) + sent, BF),
            pltpu.VMEM((2,) + held, BF),
            pltpu.VMEM((2,) + held, BF),
            pltpu.VMEM((2,) + sent, BF),
            pltpu.VMEM((2,) + held, BF),
            pltpu.VMEM((2,) + held, BF),
            pltpu.VMEM(held, BF),
            pltpu.VMEM((2,) + rows, BF),
            pltpu.VMEM((2,) + rows, BF),
            pltpu.SemaphoreType.DMA((5,)),
            pltpu.SemaphoreType.DMA((6,)),
            pltpu.SemaphoreType.DMA((6,)),
            pltpu.SemaphoreType.DMA((10,)),
            pltpu.SemaphoreType.DMA((9,)),
        ],
        compiler_params=pltpu.CompilerParams(
            collective_id=0, has_side_effects=True, vmem_limit_bytes=46 << 20
        ),
    )(
        signal.reshape(rows), gating.reshape(rows), upstream.reshape(rows),
        left_factor, right_factor,
    )
    out = pl.pallas_call(
        last_kernel,
        out_shape=(shape(rows, BF),) * 3 + (shape(square, BF),) * 2,
        in_specs=[vmem] * 7,
        out_specs=(hbm,) * 5,
        scratch_shapes=[
            pltpu.VMEM(rows, BF),
            pltpu.VMEM(rows, BF),
            pltpu.VMEM(rows, BF),
            pltpu.SemaphoreType.DMA((3, 4)),
            pltpu.SemaphoreType.DMA((2, 4)),
        ],
        compiler_params=pltpu.CompilerParams(vmem_limit_bytes=8 << 20),
    )(*[pltpu.with_memory_space_constraint(o, pltpu.VMEM) for o in last])
    return tuple(o.reshape(signal.shape) for o in out[:3]) + tuple(out[3:])


def solution(mesh):
    blocks = (P("dp", "seq", None),) * 3 + (P("seq", None, None),) * 2
    return jax.shard_map(shards, mesh=mesh, in_specs=blocks, out_specs=blocks, check_vma=False)
```

```python
import jax
import jax.numpy as jnp
from jax import lax
from jax.experimental import pallas as pl
from jax.experimental.pallas import tpu as pltpu
from jax.sharding import PartitionSpec as P

MESH = pl.DeviceIdType.MESH
BF = jnp.bfloat16
F32 = jnp.float32


def position():
    zh = lax.axis_index("dp")
    q = lax.axis_index("seq")
    return zh, q // 8, q % 8


def ring_device(pos, dz, dc):
    zh, yx, zc = pos
    z = (zh * 4 + zc // 2 + dz) % 8
    c = (zc + dc) % 2
    return (z // 4, yx * 8 + (z % 4) * 2 + c), ((dz + 1) % 4) * 2 + c


def plane_device(pos, t):
    zh, yx, zc = pos
    y = (yx // 4 + t // 4) % 4
    x = (yx + t) % 4
    return (zh, (y * 4 + x) * 8 + zc), y * 4 + x


def remote(src, dst, send, recv, device):
    return pltpu.make_async_remote_copy(
        src_ref=src, dst_ref=dst, send_sem=send, recv_sem=recv,
        device_id=device, device_id_type=MESH,
    )


def wait_bytes(ref, sem):
    pltpu.make_async_copy(ref, ref, sem).wait()


def dot(a, b, ca, cb):
    return lax.dot_general(a, b, (((ca,), (cb,)), ((), ())), preferred_element_type=F32)


def pack_matrix():
    r = lax.broadcasted_iota(jnp.int32, (256, 256), 0)
    c = lax.broadcasted_iota(jnp.int32, (256, 256), 1)
    want = ((r // 4) % 4) * 64 + (r // 16) * 4 + r % 4
    return jnp.where(c == want, 1.0, 0.0).astype(BF)


def unpack_matrix():
    r = lax.broadcasted_iota(jnp.int32, (256, 256), 0)
    c = lax.broadcasted_iota(jnp.int32, (256, 256), 1)
    want = ((r // 4) % 16) * 16 + (r % 4) * 4 + r // 64
    return jnp.where(c == want, 1.0, 0.0).astype(BF)


def unpack(perm, src, dst):
    for b in range(8):
        rows = jnp.concatenate(
            [src[:, 2 * b].reshape(128, 256), src[:, 2 * b + 1].reshape(128, 256)], axis=0
        )
        flat = dot(perm[1], rows, 1, 0).astype(BF).reshape(4, 64, 256)
        for n in range(4):
            dst[n, pl.ds(64 * b, 64)] = flat[n]


def kernel(
    v_hbm, g_hbm, u_hbm, l_hbm, r_hbm,
    b3, perm, gate, up, gsignal, gleft, gright,
    vals, left, right, work, mixed,
    s2, a2, b2, s1, a1, b1, s4, a4, b4, a3,
    cols, gcols, load, xs, xr, zs, zr,
):
    pos = position()
    zh, yx, zc = pos
    other = 1 - zh
    z = zh * 4 + zc // 2
    here = 2 + zc % 2
    lanes = [((j - zc // 2 + 5) % 4) * 2 for j in range(4)]

    loads = [
        pltpu.make_async_copy(src, dst, load.at[n])
        for n, (src, dst) in enumerate(
            ((u_hbm, up), (g_hbm, gate), (v_hbm, vals.at[zh]), (l_hbm, left), (r_hbm, right))
        )
    ]
    for copy in loads:
        copy.start()

    barrier = pltpu.get_barrier_semaphore()

    for dz in (4, 3, 5, 2, 6, 1, 7):
        for dc in (0, 1):
            pl.semaphore_signal(
                barrier, inc=1, device_id=ring_device(pos, dz, dc)[0], device_id_type=MESH
            )
    for t in (10, 11, 14, 9, 6, 2, 8, 15, 13, 7, 5, 12, 3, 4, 1):
        pl.semaphore_signal(barrier, inc=1, device_id=plane_device(pos, t)[0], device_id_type=MESH)
    pl.semaphore_signal(barrier, inc=1, device_id=ring_device(pos, 0, 1)[0], device_id_type=MESH)

    perm[0] = pack_matrix()
    perm[1] = unpack_matrix()
    def pack(src, dst, half=None):
        for b in range(8):
            rows = jnp.concatenate([src[n, pl.ds(64 * b, 64)] for n in range(4)], axis=0)
            packed = dot(perm[0], rows, 1, 0).astype(BF).reshape(2, 4, 2, 16, 256)
            for h in range(2):
                for j in range(4):
                    if half is None:
                        dst[2 * b + h, pl.ds(lanes[j], 2)] = packed[h, j]
                    else:
                        dst[half[j], 2 * b + h, pl.ds(lanes[j], 2)] = packed[h, j]

    def plane_send(src, dst, n, width=8):
        lane = pl.ds(0, width)
        pltpu.make_async_copy(src.at[yx, lane], dst.at[lane, yx], xr.at[n]).start()

        for t in (10, 5, 15, 7, 13, 1, 4, 3, 12, 6, 9, 14, 11, 2, 8):
            device, there = plane_device(pos, t)
            remote(src.at[there, lane], dst.at[lane, yx], xs.at[n], xr.at[n], device).start()

    def ring_send(src, dst, hops, send, recv):
        for dz, dc in hops:
            device, lane = ring_device(pos, dz, dc)
            remote(src.at[lane], dst.at[zc], send, recv, device).start()

    def ring_near(a, b, n, first):
        pltpu.make_async_copy(a.at[zh, here], b.at[zh, zc], zr.at[first + zh]).start()
        ring_send(
            a.at[zh], b.at[zh], ((1, 0), (7, 0), (1, 1), (7, 1), (0, 1)),
            zs.at[n + 1], zr.at[first + zh],
        )

    def ring_far(a, b, n, first):
        ring_send(
            a.at[zh], b.at[zh], ((2, 0), (6, 0), (2, 1), (6, 1)), zs.at[n], zr.at[first + zh]
        )

    def ring_other(a, b, n, first):
        pltpu.make_async_copy(a.at[other, here], b.at[other, zc], zr.at[first + other]).start()
        ring_send(
            a.at[other], b.at[other], ((1, 0), (7, 0), (1, 1), (7, 1), (0, 1)),
            zs.at[n + 2], zr.at[first + other],
        )

    def mix(s, dst, first, last):
        @pl.loop(first, last)
        def _(n):
            dst[n] = dot(left[n], vals[s, n], 1, 0).astype(BF)

    def column_back(s):
        unpack(perm, b2.at[s], gcols.at[s])

        @pl.loop(0, 4)
        def _(k):
            work[k] = dot(right[k], gcols[s, k], 0, 0).astype(BF)

        pack(work, s4.at[s])

    def column(s):
        wait_bytes(b1.at[0], zr.at[3 + s])
        unpack(perm, b1.at[s], cols.at[s])

        @pl.loop(0, 4)
        def _(k):
            work[k] = dot(right[k], cols[s, k], 1, 0).astype(BF)

        pack(work, s1, [jnp.where(w == s, 0, 1) for w in wanted])

    loads[0].wait()
    loads[1].wait()

    @pl.loop(0, 4)
    def _(n):
        work[n] = (up[n].astype(F32) * gate[n].astype(F32)).astype(BF)

    pack(work, s2)
    pl.semaphore_wait(barrier, 30)
    partner, _ = ring_device(pos, 4, 0)

    def share_signal(first, last):
        for n in range(first, last):
            remote(v_hbm.at[n], vals.at[zh, n], zs.at[0], zr.at[8 * (n // 2)], partner).start()

    share_signal(0, 2)
    plane_send(s2, a2, 0)

    loads[2].wait()
    loads[3].wait()
    mix(zh, work, 0, 4)
    pack(work, s1.at[zh])
    plane_send(s1.at[zh], a1.at[zh], 1)

    wait_bytes(a2, xr.at[0])
    pltpu.make_async_copy(a2.at[here], b2.at[zh, zc], zr.at[1 + zh]).start()
    ring_send(
        a2, b2.at[zh],
        ((4, 0), (4, 1), (3, 0), (5, 0), (3, 1), (5, 1), (2, 0), (6, 0)),
        zs.at[1], zr.at[1 + zh],
    )
    ring_send(
        a2, b2.at[zh],
        ((2, 1), (6, 1), (1, 0), (7, 0), (1, 1), (7, 1), (0, 1)),
        zs.at[2], zr.at[1 + zh],
    )
    share_signal(2, 4)
    wait_bytes(a1.at[0], xr.at[1])
    ring_far(a1, b1, 3, 3)
    ring_near(a1, b1, 3, 3)

    loads[4].wait()
    wait_bytes(b2.at[0], zr.at[1 + zh])
    column_back(zh)
    plane_send(s4.at[zh], a4.at[zh], 3)
    wait_bytes(b2.at[0], zr.at[1 + other])
    column_back(other)
    plane_send(s4.at[other], a4.at[other], 4, 6)

    wait_bytes(vals.at[0, pl.ds(0, 2)], zr.at[0])
    mix(other, mixed, 0, 2)
    wait_bytes(vals.at[0, pl.ds(0, 2)], zr.at[8])
    mix(other, mixed, 2, 4)
    pack(mixed, s1.at[other])
    plane_send(s1.at[other], a1.at[other], 2, 6)
    wait_bytes(a1.at[0, pl.ds(0, 6)], xr.at[2])
    ring_other(a1, b1, 3, 3)
    wait_bytes(a4.at[0], xr.at[3])
    ring_far(a4, b4, 6, 5)
    ring_near(a4, b4, 6, 5)
    wait_bytes(a4.at[0, pl.ds(0, 6)], xr.at[4])
    ring_other(a4, b4, 6, 5)

    wait_bytes(s1.at[0, pl.ds(0, 15)], xs.at[1])
    wait_bytes(s1.at[0, pl.ds(0, 15), pl.ds(0, 6)], xs.at[2])
    far = jnp.where(zc % 2 == 0, 2, 6)
    wanted = []
    for j in range(4):
        hop = (j - zc // 2 + 4) % 4
        hop = jnp.where(hop == 2, far, jnp.where(hop == 3, 7, hop))
        wanted.append(((z + hop) % 8) // 4)
    column(zh)
    column(other)
    plane_send(s1.at[0], a3, 5)

    @pl.loop(0, 4)
    def _(k):
        gright[k] = (
            dot(gcols[0, k], cols[0, k], 1, 1) + dot(gcols[1, k], cols[1, k], 1, 1)
        ).astype(BF)

    wait_bytes(a3, xr.at[5])
    pltpu.make_async_copy(a3.at[here], b3.at[zc], zr.at[7]).start()
    ring_send(
        a3, b3, ((far, 0), (far, 1), (1, 0), (7, 0), (1, 1), (7, 1), (0, 1)), zs.at[9], zr.at[7]
    )

    for s in (0, 1):
        wait_bytes(b4.at[0], zr.at[5 + s])
        unpack(perm, b4.at[s], cols.at[s])

    @pl.loop(0, 4)
    def _(n):
        gsignal[n] = dot(left[n], cols[zh, n], 0, 0).astype(BF)
        gleft[n] = (
            dot(cols[0, n], vals[0, n], 1, 1) + dot(cols[1, n], vals[1, n], 1, 1)
        ).astype(BF)

    wait_bytes(b3, zr.at[7])
    wait_bytes(vals.at[0], zs.at[0])
    for n in (0, 3, 5):
        wait_bytes(s1.at[0, pl.ds(0, 15)], xs.at[n])
    wait_bytes(s1.at[0, pl.ds(0, 15), pl.ds(0, 6)], xs.at[4])
    wait_bytes(a2, zs.at[1])
    wait_bytes(a2.at[pl.ds(0, 7)], zs.at[2])
    for n in (3, 6):
        wait_bytes(a2.at[pl.ds(0, 4)], zs.at[n])
        wait_bytes(a2.at[pl.ds(0, 5)], zs.at[n + 1])
        wait_bytes(a2.at[pl.ds(0, 5)], zs.at[n + 2])
    wait_bytes(a3.at[pl.ds(0, 7)], zs.at[9])


def last_kernel(
    b3, perm, gate, up, gsignal, gleft, gright,
    out_hbm, gg_hbm, gs_hbm, gl_hbm, gr_hbm,
    second, out, ggate, sem, out_sem,
):
    copies = [
        pltpu.make_async_copy(src, dst, sem.at[n])
        for n, (src, dst) in enumerate(((gright, gr_hbm), (gleft, gl_hbm), (gsignal, gs_hbm)))
    ]
    for copy in copies:
        copy.start()
    unpack(perm, b3, second)
    for n in range(4):
        wide = second[n].astype(F32)
        out[n] = (gate[n].astype(F32) * wide).astype(BF)
        ggate[n] = (up[n].astype(F32) * wide).astype(BF)
        for k, (src, dst) in enumerate(((out, out_hbm), (ggate, gg_hbm))):
            copies.append(pltpu.make_async_copy(src.at[n], dst.at[n], out_sem.at[k, n]))
            copies[-1].start()
    for copy in copies:
        copy.wait()


def shards(signal, gating, upstream, left_factor, right_factor):
    rows = (4, 512, 256)
    square = (4, 512, 512)
    sent = (16, 8, 16, 256)
    held = (8, 16, 16, 256)
    hbm = pl.BlockSpec(memory_space=pl.ANY)
    vmem = pl.BlockSpec(memory_space=pltpu.VMEM)
    shape = jax.ShapeDtypeStruct
    last = pl.pallas_call(
        kernel,
        out_shape=(
            pltpu.VMEM(held, BF),
            pltpu.VMEM((2, 256, 256), BF),
            pltpu.VMEM(rows, BF),
            pltpu.VMEM(rows, BF),
            pltpu.VMEM(rows, BF),
            pltpu.VMEM(square, BF),
            pltpu.VMEM(square, BF),
        ),
        in_specs=[hbm] * 5,
        out_specs=(vmem,) * 7,
        scratch_shapes=[
            pltpu.VMEM((2,) + rows, BF),
            pltpu.VMEM(square, BF),
            pltpu.VMEM(square, BF),
            pltpu.VMEM(rows, BF),
            pltpu.VMEM(rows, BF),
            pltpu.VMEM(sent, BF),
            pltpu.VMEM(held, BF),
            pltpu.VMEM((2,) + held, BF),
            pltpu.VMEM((2,) + sent, BF),
            pltpu.VMEM((2,) + held, BF),
            pltpu.VMEM((2,) + held, BF),
            pltpu.VMEM((2,) + sent, BF),
            pltpu.VMEM((2,) + held, BF),
            pltpu.VMEM((2,) + held, BF),
            pltpu.VMEM(held, BF),
            pltpu.VMEM((2,) + rows, BF),
            pltpu.VMEM((2,) + rows, BF),
            pltpu.SemaphoreType.DMA((5,)),
            pltpu.SemaphoreType.DMA((6,)),
            pltpu.SemaphoreType.DMA((6,)),
            pltpu.SemaphoreType.DMA((10,)),
            pltpu.SemaphoreType.DMA((9,)),
        ],
        compiler_params=pltpu.CompilerParams(
            collective_id=0, has_side_effects=True, vmem_limit_bytes=46 << 20
        ),
    )(
        signal.reshape(rows), gating.reshape(rows), upstream.reshape(rows),
        left_factor, right_factor,
    )
    out = pl.pallas_call(
        last_kernel,
        out_shape=(shape(rows, BF),) * 3 + (shape(square, BF),) * 2,
        in_specs=[vmem] * 7,
        out_specs=(hbm,) * 5,
        scratch_shapes=[
            pltpu.VMEM(rows, BF),
            pltpu.VMEM(rows, BF),
            pltpu.VMEM(rows, BF),
            pltpu.SemaphoreType.DMA((3,)),
            pltpu.SemaphoreType.DMA((2, 4)),
        ],
        compiler_params=pltpu.CompilerParams(vmem_limit_bytes=8 << 20),
    )(*[pltpu.with_memory_space_constraint(o, pltpu.VMEM) for o in last])
    return tuple(o.reshape(signal.shape) for o in out[:3]) + tuple(out[3:])


def solution(mesh):
    blocks = (P("dp", "seq", None),) * 3 + (P("seq", None, None),) * 2
    return jax.shard_map(shards, mesh=mesh, in_specs=blocks, out_specs=blocks, check_vma=False)
```
